32 devices in a mesh: bulk: 8 (over z, x), tp: 4 (over y, core).
Axes of the slice: x: 2, y: 2, z: 4, core: 2. Of those that a mesh axis runs over, the one named last changes fastest.
Arguments:
- queries: bfloat16 [8192, 8192], P('bulk', 'tp'), may hold values from -40 to 40, as said below
- comp_keys: bfloat16 [8192, 1024], P(('bulk', 'tp')), may hold values from -8 to 8
- comp_values: bfloat16 [8192, 1024], P(('bulk', 'tp')), may hold values from -6 to 6
- prefix_keys: bfloat16 [8, 2048, 1024], P('bulk', 'tp'), may hold values from -10 to 10
- prefix_values: bfloat16 [8, 2048, 1024], P('bulk', 'tp'), may hold values from -6 to 6
- lengths: int32 [8, 16], P('bulk'), may hold values from 1 to 64, as said below
- routing: int32 [8, 64], P('bulk'), may hold values from 0 to 7, as said below
- residual: bfloat16 [8192, 8192], P('bulk', 'tp'), may hold values from -6 to 6
- out_weight: bfloat16 [8192, 8192], P('tp'), may hold values from -0.09375 to 0.09375
Outputs:
- mixed: bfloat16 [4096, 8192], P('bulk', 'tp')
The draws below stay inside these ranges and needn't reach their ends.
Inputs may be any that keep to these rules, and one draw needn't show every extreme that they name: queries are of order one except on some rows of the hidden draw. `lengths`: for every prompt, the sum over its completions of ceil(length / 8) is at most 64, and it equals 64 for some prompt in every draw. `routing`: in every row, each index of bulk appears exactly 8 times.
All inputs are finite; a program needn't handle non-finite values.
Results may differ from the reference program's by a relative error of at most 0.009.
Values may be sent and summed in bfloat16 or wider, within the bound.
No kernel may reach another device: no remote copies, remote signals or barrier semaphores. Data moves between devices by JAX's collectives and lax.ppermute only.
A program may use at most 128 MiB of HBM per device.

```python
import math
import jax
import jax.numpy as jnp
from jax import lax

D = 8192
HEADS = 64
KVH = 8
HD = 128
PLEN = 2048
CMAX = 64
GROUP = 16
BLK = 8
SLOTS = 64
PROMPTS = 8
HOME = 1024
ROWS = 8192
CAP = 8
N_BULK = 8
N_TP = 4


def prefix_base(key):
    values_raw = jax.random.normal(jax.random.fold_in(key, 101), (PROMPTS, PLEN, KVH * HD), jnp.float32)
    return jnp.clip(values_raw, -4.0, 4.0)


def draw_prefix_keys(key, part):
    values_raw = prefix_base(key)
    return values_raw.astype(jnp.bfloat16)


def draw_queries(key, part):
    values_raw = jax.random.normal(jax.random.fold_in(key, 202), (ROWS, HEADS * HD), jnp.float32)
    values_raw = 2.5 * jnp.clip(values_raw, -4.0, 4.0)
    return values_raw.astype(jnp.bfloat16)


def draw_lengths(key, part):
    per_comp = CMAX // BLK
    base_key = jax.random.fold_in(key, 303)
    extra_room = SLOTS - GROUP
    picks = jax.random.randint(jax.random.fold_in(base_key, 1), (PROMPTS,), 0, extra_room + 1)
    totals = picks * picks // max(extra_room, 1)
    fullest = jax.random.randint(jax.random.fold_in(base_key, 2), (), 0, PROMPTS)
    prompt_ids = jnp.arange(PROMPTS, dtype=jnp.int32)
    totals = jnp.where(prompt_ids == fullest, extra_room, totals)
    favoured = jax.random.randint(jax.random.fold_in(base_key, 5), (), 0, GROUP)
    spare = GROUP * (per_comp - 1)
    prompt_keys = jax.random.split(jax.random.fold_in(base_key, 3), PROMPTS)
    ranking = jax.vmap(lambda single: jax.random.permutation(single, spare))(prompt_keys).astype(jnp.int32)
    owner = jnp.arange(spare, dtype=jnp.int32) // (per_comp - 1)
    boosted = (prompt_ids[:, None] == fullest) & (owner[None, :] == favoured)
    order_key = ranking - jnp.where(boosted, spare, 0).astype(jnp.int32)
    position = jnp.argsort(jnp.argsort(order_key, axis=1), axis=1).astype(jnp.int32)
    chosen = position < totals[:, None]
    members = chosen[:, :, None] & (owner[None, :, None] == jnp.arange(GROUP, dtype=jnp.int32)[None, None, :])
    extra = jnp.sum(members.astype(jnp.int32), axis=1)
    tail_rows = jax.random.randint(jax.random.fold_in(base_key, 4), (PROMPTS, GROUP), 1, BLK + 1)
    full_one = (prompt_ids[:, None] == fullest) & (jnp.arange(GROUP, dtype=jnp.int32)[None, :] == favoured)
    tail_rows = jnp.where(full_one, BLK, tail_rows)
    return (extra * BLK + tail_rows).astype(jnp.int32)


def draw_routing(key, part):
    prompt_keys = jax.random.split(jax.random.fold_in(key, 404), PROMPTS)
    shuffled = jax.vmap(lambda single: jax.random.permutation(single, SLOTS))(prompt_keys)
    return (shuffled // CAP).astype(jnp.int32)


def with_spikes(array, key, source, target, parts, factor):
    owner, partner = [(jnp.arange(array.shape[dim]) // (array.shape[dim] // parts)).reshape([-1 if axis == dim else 1 for axis in range(array.ndim)]) for dim in (source, target)]
    chosen = jax.random.permutation(key, parts)[partner]
    strong = (owner == chosen) | (owner == (partner + parts // 2) % parts)
    return jnp.where(strong, factor * array, array)


def block_scale(rng, dims, shards, smallest, largest):
    gain = 1.0
    for dim, shards_of in shards:
        heights = jax.random.uniform(jax.random.fold_in(jax.random.fold_in(rng, 6), dim), (shards_of,), jnp.float32, smallest / len(shards), largest / len(shards))
        gain = gain * jnp.repeat(jnp.exp(heights), dims[dim] // shards_of).reshape((-1,) + (1,) * (len(dims) - 1 - dim))
    return gain


def gaussian(stream_key, extent, spread, most, pieces=(), kind=jnp.bfloat16):
    drawn = jax.random.normal(stream_key, extent, jnp.float32) * spread
    if len(pieces) > 0:
        drawn = block_scale(stream_key, extent, pieces, -0.22, 0.18) * drawn
    return jnp.clip(drawn, min=-most, max=most).astype(kind)


def bell_draw_with(rng, shape, scale, limit, shards, heavy, kind=jnp.bfloat16):
    array = scale * jax.random.normal(rng, shape, jnp.float32)
    if shards:
        array = array * block_scale(rng, shape, shards, -0.22, 0.18)
    return jnp.clip(with_spikes(array, jax.random.fold_in(rng, 3), *heavy), -limit, limit).astype(kind)


def setup_inputs(seed: int = 0) -> dict:
    arg_keys = jax.random.split(jax.random.key(seed), 10)
    return {
        "queries": draw_queries(jax.random.fold_in(arg_keys[9], 71), 0),
        "comp_keys": gaussian(arg_keys[1], (ROWS, KVH * HD), 1.4, 8.0, ((0, 32),)),
        "comp_values": gaussian(arg_keys[2], (ROWS, KVH * HD), 1.0, 6.0, ((0, 32),)),
        "prefix_keys": draw_prefix_keys(jax.random.fold_in(arg_keys[9], 71), 0),
        "prefix_values": gaussian(arg_keys[4], (PROMPTS, PLEN, KVH * HD), 1.0, 6.0, ((0, 8), (1, 4))),
        "lengths": draw_lengths(jax.random.fold_in(arg_keys[9], 71), 0),
        "routing": draw_routing(jax.random.fold_in(arg_keys[9], 71), 0),
        "residual": gaussian(arg_keys[7], (ROWS, D), 1.0, 6.0, ((0, 8), (1, 4))),
        "out_weight": bell_draw_with(arg_keys[8], (HEADS * HD, D), (HEADS * HD) ** -0.5, 0.09375, ((0, 4),), (0, 1, 4, 2.0)),
    }


def tables(lens_row, route_row, per_pair):
    per_comp = CMAX // BLK
    counts = ((lens_row + BLK - 1) // BLK).astype(jnp.int32)
    inner = jnp.arange(per_comp, dtype=jnp.int32)
    live_flags = (inner[None, :] < counts[:, None]).reshape(-1).astype(jnp.int32)
    live_rank = (jnp.cumsum(live_flags) - 1).astype(jnp.int32)
    block_total = live_flags.shape[0]
    slot_order = jnp.arange(SLOTS, dtype=jnp.int32)
    rank_hits = (live_rank[:, None] == slot_order[None, :]) & (live_flags[:, None] == 1)
    block_ids = jnp.arange(block_total, dtype=jnp.int32)
    block_of = lax.optimization_barrier(jnp.sum(jnp.where(rank_hits, block_ids[:, None], 0), axis=0)).astype(jnp.int32)
    slot_used = jnp.any(rank_hits, axis=0)
    same_dest = route_row[:, None] == route_row[None, :]
    earlier = slot_order[None, :] < slot_order[:, None]
    slot_place = (route_row * per_pair + lax.optimization_barrier(jnp.sum(same_dest & earlier, axis=1))).astype(jnp.int32)
    place_hits = slot_place[None, :] == slot_order[:, None]
    block_for = lax.optimization_barrier(jnp.sum(jnp.where(place_hits, block_of[None, :], 0), axis=1)).astype(jnp.int32)
    live_for = jnp.any(place_hits & slot_used[None, :], axis=1)
    return (block_for, live_for)

def attend(query_blk, key_own, value_own, key_pre, value_pre, lens_blk):
    inv_root = 1.0 / math.sqrt(query_blk.shape[-1])
    query_f = query_blk.astype(jnp.float32)
    score_pre = jnp.einsum('bckqh,pkh->bckqp', query_f, key_pre.astype(jnp.float32)) * inv_root
    score_own = jnp.einsum('bckqh,bekh->bckqe', query_f, key_own.astype(jnp.float32)) * inv_root
    positions = jnp.arange(query_blk.shape[1], dtype=jnp.int32)
    causal = positions[None, :] <= positions[:, None]
    score_own = jnp.where(causal[None, :, None, None, :], score_own, jnp.float32(-1e+30))
    top_score = jnp.maximum(lax.optimization_barrier(jnp.max(score_pre, axis=-1)), lax.optimization_barrier(jnp.max(score_own, axis=-1)))
    expo_pre = jnp.exp(score_pre - top_score[..., None])
    expo_own = jnp.exp(score_own - top_score[..., None])
    total = lax.optimization_barrier(jnp.sum(expo_pre, axis=-1)) + lax.optimization_barrier(jnp.sum(expo_own, axis=-1))
    weight_pre = lax.optimization_barrier(expo_pre.astype(jnp.bfloat16)).astype(jnp.float32)
    weight_own = lax.optimization_barrier(expo_own.astype(jnp.bfloat16)).astype(jnp.float32)
    summed = jnp.einsum('bckqp,pkh->bckqh', weight_pre, value_pre.astype(jnp.float32))
    summed = summed + jnp.einsum('bckqe,bekh->bckqh', weight_own, value_own.astype(jnp.float32))
    result = summed / total[..., None]
    valid = positions[None, :] < lens_blk[:, None]
    result = jnp.where(valid[:, :, None, None, None], result, jnp.float32(0.0))
    return result.astype(jnp.bfloat16)

def reference(queries, comp_keys, comp_values, prefix_keys, prefix_values, lengths, routing, residual, out_weight):
    group_size = HEADS // KVH
    per_pair = SLOTS // N_BULK
    block_total = HOME // BLK
    width_loc = HEADS * HD // N_TP
    query_all = queries.reshape(PROMPTS, GROUP, CMAX, KVH, group_size, HD)
    keys_all = comp_keys.reshape(PROMPTS, GROUP, CMAX, KVH, HD)
    values_all = comp_values.reshape(PROMPTS, GROUP, CMAX, KVH, HD)
    prekeys_all = prefix_keys.reshape(PROMPTS, PLEN, KVH, HD)
    prevalues_all = prefix_values.reshape(PROMPTS, PLEN, KVH, HD)
    resid_all = residual.reshape(PROMPTS, HOME, D)
    weight_parts = out_weight.reshape(N_TP, width_loc, D)

    def one_prompt(bundle):
        query_p, keys_p, values_p, prekeys_p, prevalues_p, lens_p, route_p, resid_p = bundle

        def one_completion(inner_bundle):
            query_c, keys_c, values_c, lens_c = inner_bundle
            return attend(query_c[None], keys_c[None], values_c[None], prekeys_p, prevalues_p, lens_c[None])[0]
        context = lax.map(one_completion, (query_p, keys_p, values_p, lens_p))
        context = context.reshape(HOME, HEADS * HD)
        summed = jnp.zeros((HOME, D), jnp.float32)
        for shard_index in range(N_TP):
            piece = jnp.dot(context[:, shard_index * width_loc:(shard_index + 1) * width_loc], weight_parts[shard_index], preferred_element_type=jnp.float32)
            summed = summed + lax.optimization_barrier(piece.astype(jnp.bfloat16)).astype(jnp.float32)
        row_ids = jnp.arange(HOME, dtype=jnp.int32)
        row_valid = row_ids % CMAX < lens_p[row_ids // CMAX]
        finished = jnp.where(row_valid[:, None], resid_p.astype(jnp.float32) + summed, jnp.float32(0.0)).astype(jnp.bfloat16)
        block_for, live_for = tables(lens_p, route_p, per_pair)
        picked = jnp.take(finished.reshape(block_total, BLK, D), block_for, axis=0)
        return jnp.where(live_for[:, None, None], picked, jnp.zeros((), jnp.bfloat16))
    sent = lax.map(one_prompt, (query_all, keys_all, values_all, prekeys_all, prevalues_all, lengths, routing, resid_all))
    sent = sent.reshape(PROMPTS, N_BULK, per_pair, BLK, D)
    sent = jnp.transpose(sent, (1, 0, 2, 3, 4))
    return sent.reshape(N_BULK * SLOTS * BLK, D)
```

```python
import functools
import math

import jax
import jax.numpy as jnp
from jax import lax
from jax.experimental import pallas as pl
from jax.experimental.pallas import tpu as pltpu
from jax.sharding import PartitionSpec as P

HEADS = 64
KVH = 8
HD = 128
CMAX = 64
GROUP = 16
BLK = 8
SLOTS = 64
LIVE = SLOTS * BLK
HOME = GROUP * CMAX
NEG = -1e30
CHUNKS = 4
ATT_ROWS = 128
ATT_SUB = 4
VMEM = 60 << 20


def dot_nt(a, b):
    return lax.dot_general(a, b, (((1,), (1,)), ((), ())), preferred_element_type=jnp.float32)


def dot_nn(a, b):
    return jnp.dot(a, b, preferred_element_type=jnp.float32)


def attend(q, bias, src_row, pieces, pre, own, kv_head, per_kv):
    rows, sub = ATT_ROWS, ATT_SUB
    window = rows + CMAX
    width = per_kv * HD
    count = len(pieces)
    heads = per_kv // sub
    fold = math.log2(math.e) / math.sqrt(HD)

    def kernel(q_ref, bias_ref, src_ref, *rest):
        refs = rest[:count]
        o_ref, own_k, own_v = rest[count:]
        step = pl.program_id(0)

        @pl.when(step == 0)
        def _():
            hit = lax.broadcasted_iota(jnp.int32, (LIVE, HOME), 0) == src_ref[...]
            pick = jnp.where(hit, 1.0, 0.0).astype(jnp.bfloat16)
            raw_k = jnp.concatenate([r[2 * pre : 2 * pre + own, :] for r in refs], 0)
            raw_v = jnp.concatenate([r[2 * pre + own :, :] for r in refs], 0)
            own_k[0:CMAX, :] = jnp.zeros((CMAX, HD), jnp.bfloat16)
            own_v[0:CMAX, :] = jnp.zeros((CMAX, HD), jnp.bfloat16)
            own_k[CMAX:, :] = dot_nn(pick, raw_k).astype(jnp.bfloat16)
            own_v[CMAX:, :] = dot_nn(pick, raw_v).astype(jnp.bfloat16)

        start = pl.multiple_of(step * rows, CMAX)
        near_k = own_k[pl.ds(start, window), :]
        near_v = own_v[pl.ds(start, window), :]
        mask = jnp.concatenate([bias_ref[...]] * heads, 0)
        for part in range(sub):
            cols = [slice(h * HD, (h + 1) * HD) for h in range(part * heads, (part + 1) * heads)]
            query = jnp.concatenate([q_ref[:, c] for c in cols], 0)
            far = [dot_nt(query, r[0:pre, :]) for r in refs]
            near = dot_nt(query, near_k) + mask
            top = jnp.max(near, axis=1, keepdims=True)
            for s in far:
                top = jnp.maximum(top, jnp.max(s, axis=1, keepdims=True))
            top = top * fold
            expo = jnp.exp2(near * fold - top)
            total = jnp.sum(expo, axis=1, keepdims=True)
            acc = dot_nn(expo.astype(jnp.bfloat16), near_v)
            for s, r in zip(far, refs):
                expo = jnp.exp2(s * fold - top)
                total = total + jnp.sum(expo, axis=1, keepdims=True)
                acc = acc + dot_nn(expo.astype(jnp.bfloat16), r[pre : 2 * pre, :])
            out = (acc / total).astype(jnp.bfloat16)
            for k, c in enumerate(cols):
                o_ref[:, c] = out[k * rows : (k + 1) * rows, :]

    whole = lambda a: pl.BlockSpec(a.shape, lambda i: (0, 0))
    return pl.pallas_call(
        kernel,
        grid=(LIVE // rows,),
        in_specs=[
            pl.BlockSpec((rows, width), lambda i: (i, kv_head)),
            pl.BlockSpec((rows, window), lambda i: (i, 0)),
            whole(src_row),
        ]
        + [whole(p) for p in pieces],
        out_specs=pl.BlockSpec((rows, width), lambda i: (i, 0)),
        out_shape=jax.ShapeDtypeStruct((LIVE, width), jnp.bfloat16),
        scratch_shapes=[pltpu.VMEM((CMAX + LIVE, HD), jnp.bfloat16)] * 2,
        compiler_params=pltpu.CompilerParams(
            dimension_semantics=("arbitrary",), vmem_limit_bytes=VMEM
        ),
        name="attend",
    )(q, bias, src_row, *pieces)


def project(contexts, weight, blocks, tile, extras, wide):
    groups, tiles = blocks.shape
    count = len(contexts)
    depth = contexts[0].shape[1]

    def kernel(blocks_ref, *refs):
        ctx = refs[:count]
        w_ref = refs[count]
        more = refs[count + 1 : -1]
        o_ref = refs[-1]
        acc = dot_nn(ctx[0][...], w_ref[0:depth, :])
        for i in range(1, count):
            acc = acc + dot_nn(ctx[i][...], w_ref[i * depth : (i + 1) * depth, :])
        acc = acc.astype(jnp.bfloat16)
        if more:
            acc = acc.astype(jnp.float32)
            for r in more:
                acc = acc + r[0].astype(jnp.float32)
        o_ref[0] = acc.astype(o_ref.dtype)

    def extra_spec(lead, col):
        return pl.BlockSpec((1, LIVE, tile), lambda g, n, b: (lead + g, 0, col + n))

    return pl.pallas_call(
        kernel,
        grid_spec=pltpu.PrefetchScalarGridSpec(
            num_scalar_prefetch=1,
            grid=(groups, tiles),
            in_specs=[pl.BlockSpec((LIVE, depth), lambda g, n, b: (0, 0))] * count
            + [pl.BlockSpec((weight.shape[0], tile), lambda g, n, b: (0, b[g, n]))]
            + [extra_spec(lead, col) for _, lead, col in extras],
            out_specs=pl.BlockSpec((1, LIVE, tile), lambda g, n, b: (g, 0, n)),
        ),
        out_shape=jax.ShapeDtypeStruct(
            (groups, LIVE, tiles * tile), jnp.float32 if wide else jnp.bfloat16
        ),
        compiler_params=pltpu.CompilerParams(
            dimension_semantics=("arbitrary", "arbitrary"), vmem_limit_bytes=VMEM
        ),
        name="project",
    )(blocks, *contexts, weight, *[e for e, _, _ in extras])


def local(
    queries,
    comp_keys,
    comp_values,
    prefix_keys,
    prefix_values,
    lengths,
    routing,
    residual,
    out_weight,
):
    tp_count = lax.axis_size("tp")
    bulk_count = lax.axis_size("bulk")
    me = lax.axis_index("tp")
    group_size = HEADS // KVH
    heads_loc = HEADS // tp_count
    kv_local = max(1, heads_loc // group_size)
    per_kv = heads_loc // kv_local
    cap = SLOTS // bulk_count
    width_loc = residual.shape[1]
    pre = prefix_keys.shape[1]
    own = comp_keys.shape[0]

    shelf = jnp.concatenate([prefix_keys[0], prefix_values[0], comp_keys, comp_values], 0)

    def piece(peer, inner):
        col = ((peer * heads_loc) // group_size + inner) * HD
        return lax.dynamic_slice(shelf, (0, col), (shelf.shape[0], HD))

    pieces = []
    for inner in range(kv_local):
        got = [piece(me, inner)]
        for r in range(1, tp_count):
            got.append(
                lax.ppermute(piece(me ^ r, inner), "tp", [(t, t ^ r) for t in range(tp_count)])
            )
        pieces.append(got)

    lens = lengths.reshape(GROUP, 1)
    spans = (lens + BLK - 1) // BLK * BLK
    ids = jnp.arange(GROUP, dtype=jnp.int32)
    first = jnp.sum(
        jnp.where(ids[None, :] < ids[:, None], spans.reshape(1, GROUP), 0), axis=1, keepdims=True
    )

    def packed_of(row):
        hit = ids[:, None] == row // CMAX
        base = jnp.sum(jnp.where(hit, first, 0), axis=0, keepdims=True)
        span = jnp.sum(jnp.where(hit, spans, 0), axis=0, keepdims=True)
        inside = row % CMAX
        return jnp.where(inside < span, base + inside, -1)

    home = jnp.arange(HOME, dtype=jnp.int32)[None, :]
    live = jnp.arange(LIVE, dtype=jnp.int32)
    packed_home = packed_of(home)
    packed_near = packed_of((home // own ^ me) * own + home % own)
    pick = (live[:, None] == packed_home).astype(jnp.bfloat16)

    within = (live[None, :] >= first) & (live[None, :] < first + lens)
    valid = jnp.any(within, axis=0, keepdims=True)
    route = routing.reshape(SLOTS)
    slot = jnp.arange(SLOTS, dtype=jnp.int32)
    before = (route[:, None] == route[None, :]) & (slot[None, :] < slot[:, None])
    place = route[:, None] * cap + jnp.sum(before, axis=1, keepdims=True, dtype=jnp.int32)
    place_row = jnp.sum(
        jnp.where(slot[:, None] == live[None, :] // BLK, place, 0), axis=0, keepdims=True
    )
    place_row = jnp.where(valid, place_row * BLK + live[None, :] % BLK, -1)
    order = (live[:, None] == place_row).astype(jnp.bfloat16)

    origin = jnp.max(
        jnp.where(first.reshape(1, GROUP) <= live[:, None], first.reshape(1, GROUP), 0),
        axis=1,
        keepdims=True,
    )
    window = ATT_ROWS + CMAX
    key_at = (live // ATT_ROWS * ATT_ROWS - CMAX)[:, None] + jnp.arange(window, dtype=jnp.int32)
    bias = jnp.where((key_at >= origin) & (key_at <= live[:, None]), 0.0, NEG)

    query = dot_nn(pick, queries).astype(jnp.bfloat16)
    kept = dot_nn(dot_nn(order, pick).astype(jnp.bfloat16), residual).astype(jnp.bfloat16)
    contexts = []
    for inner in range(kv_local):
        ctx = attend(query, bias, packed_near, pieces[inner], pre, own, inner, per_kv)
        contexts.append(dot_nn(order, ctx).astype(jnp.bfloat16))

    def send_home(rows):
        return lax.all_to_all(
            rows.reshape(bulk_count, -1, rows.shape[-1]),
            "bulk",
            split_axis=0,
            concat_axis=0,
            tiled=True,
        ).reshape(rows.shape)

    chunks = CHUNKS if tp_count == 4 else 1
    part = width_loc // chunks
    tile = min(512, part)
    tiles = part // tile
    per_dev = width_loc // tile
    if tp_count != 4:
        base = jnp.arange(tp_count * per_dev, dtype=jnp.int32)[None, :]
        full = project(contexts, out_weight, base, tile, [], False)[0]
        summed = lax.psum_scatter(full, "tp", scatter_dimension=1, tiled=True)
        return send_home((summed.astype(jnp.float32) + kept).astype(jnp.bfloat16))

    swap = [(t, t ^ 1) for t in range(tp_count)]
    cross = [(t, t ^ 2) for t in range(tp_count)]
    outs = []
    for j in range(chunks):
        cols = lambda *rel: jnp.stack(
            [(me ^ r) * per_dev + j * tiles + jnp.arange(tiles, dtype=jnp.int32) for r in rel]
        )
        away = project(contexts, out_weight, cols(1, 3), tile, [], False)
        near = lax.ppermute(away, "tp", swap)
        far = project(contexts, out_weight, cols(2), tile, [(near, 1, 0)], False)
        far = lax.ppermute(far, "tp", cross)
        mine = project(
            contexts, out_weight, cols(0), tile, [(near, 0, 0), (kept[None], 0, j * tiles)], True
        )
        done = (mine[0] + far[0].astype(jnp.float32)).astype(jnp.bfloat16)
        outs.append(send_home(done))
    return jnp.concatenate(outs, axis=1)


def solution(mesh):
    return jax.shard_map(
        local,
        mesh=mesh,
        in_specs=(
            P("bulk", "tp"),
            P(("bulk", "tp"), None),
            P(("bulk", "tp"), None),
            P("bulk", "tp", None),
            P("bulk", "tp", None),
            P("bulk", None),
            P("bulk", None),
            P("bulk", "tp"),
            P("tp", None),
        ),
        out_specs=P("bulk", "tp"),
        check_vma=False,
    )
```

```python
import math

import jax
import jax.numpy as jnp
from jax import lax
from jax.experimental import pallas as pl
from jax.experimental.pallas import tpu as pltpu
from jax.sharding import PartitionSpec as P


HEADS = 64
KVH = 8
HD = 128
CMAX = 64
GROUP = 16
BLK = 8
SLOTS = 64
LIVE = SLOTS * BLK
HOME = GROUP * CMAX
NEG = -1e30
CHUNKS = 2
PLAN = ("away0", "kept", "far0", "away1", "mine0", "far1", "done0", "mine1", "done1")
ATT_ROWS = 256
VMEM = 60 << 20


def dot_nt(a, b):
    return lax.dot_general(a, b, (((1,), (1,)), ((), ())), preferred_element_type=jnp.float32)


def dot_nn(a, b):
    return jnp.dot(a, b, preferred_element_type=jnp.float32)


def soft(query, parts, fold):
    scores = [dot_nt(query, k) if m is None else dot_nt(query, k) + m for k, _, m in parts]
    top = jnp.max(scores[0], axis=1, keepdims=True)
    for s in scores[1:]:
        top = jnp.maximum(top, jnp.max(s, axis=1, keepdims=True))
    top = top * fold
    acc = None
    for s, (_, v, _) in zip(scores, parts):
        expo = jnp.exp2(s * fold - top).astype(jnp.bfloat16)
        more = dot_nn(expo, jnp.concatenate([v, jnp.ones(v.shape, v.dtype)], 1))
        acc = more if acc is None else acc + more
    return acc, top


def attend_first(q, pieces, pre, kv_head, per_kv):
    rows = ATT_ROWS
    width = per_kv * HD
    count = len(pieces)
    fold = math.log2(math.e) / math.sqrt(HD)

    def kernel(q_ref, *rest):
        refs = rest[:count]
        o_ref, s_ref = rest[count:]
        lane = lax.broadcasted_iota(jnp.int32, (rows, HD), 1)
        stats = jnp.zeros((rows, HD), jnp.float32)
        for h in range(per_kv):
            c = slice(h * HD, (h + 1) * HD)
            acc, top = soft(
                q_ref[:, c], [(r[0:pre, :], r[pre : 2 * pre, :], None) for r in refs], fold
            )
            o_ref[:, c] = acc[:, :HD]
            stats = jnp.where(lane == h, top, stats)
            stats = jnp.where(lane == per_kv + h, acc[:, HD:], stats)
        s_ref[...] = stats

    whole = lambda a: pl.BlockSpec(a.shape, lambda i: (0, 0))
    return pl.pallas_call(
        kernel,
        grid=(LIVE // rows,),
        in_specs=[pl.BlockSpec((rows, width), lambda i: (i, kv_head))] + [whole(p) for p in pieces],
        out_specs=(
            pl.BlockSpec((rows, width), lambda i: (i, 0)),
            pl.BlockSpec((rows, HD), lambda i: (i, 0)),
        ),
        out_shape=(
            jax.ShapeDtypeStruct((LIVE, width), jnp.float32),
            jax.ShapeDtypeStruct((LIVE, HD), jnp.float32),
        ),
        compiler_params=pltpu.CompilerParams(
            dimension_semantics=("arbitrary",), vmem_limit_bytes=VMEM
        ),
        name="attend_first",
    )(q, *pieces)


def attend_rest(q, bias, src_row, carry, firsts, pieces, pre, own, kv_head, per_kv):
    rows = ATT_ROWS
    window = rows + CMAX
    width = per_kv * HD
    count, lead = len(pieces), len(firsts)
    fold = math.log2(math.e) / math.sqrt(HD)
    steps = LIVE // rows

    def kernel(q_ref, bias_ref, src_ref, acc_ref, stat_ref, *rest):
        head = rest[:lead]
        refs = rest[lead : lead + count]
        o_ref, own_k, own_v = rest[lead + count :]
        step = pl.program_id(0)

        @pl.when(step == 0)
        def _():
            hit = lax.broadcasted_iota(jnp.int32, (LIVE, HOME), 0) == src_ref[...]
            pick = jnp.where(hit, 1.0, 0.0).astype(jnp.bfloat16)
            raw_k = jnp.concatenate(
                [r[...][:own] for r in head] + [r[2 * pre : 2 * pre + own, :] for r in refs], 0
            )
            raw_v = jnp.concatenate(
                [r[...][own:] for r in head] + [r[2 * pre + own :, :] for r in refs], 0
            )
            own_k[0:CMAX, :] = jnp.zeros((CMAX, HD), jnp.bfloat16)
            own_v[0:CMAX, :] = jnp.zeros((CMAX, HD), jnp.bfloat16)
            own_k[CMAX:, :] = dot_nn(pick, raw_k).astype(jnp.bfloat16)
            own_v[CMAX:, :] = dot_nn(pick, raw_v).astype(jnp.bfloat16)

        start = pl.multiple_of(step * rows, CMAX)
        near_k = own_k[pl.ds(start, window), :]
        near_v = own_v[pl.ds(start, window), :]
        mask = bias_ref[...]
        stats = stat_ref[...]
        for h in range(per_kv):
            c = slice(h * HD, (h + 1) * HD)
            parts = [(near_k, near_v, mask)]
            parts += [(r[0:pre, :], r[pre : 2 * pre, :], None) for r in refs]
            acc, top = soft(q_ref[:, c], parts, fold)
            old_top = stats[:, h : h + 1]
            old_total = stats[:, per_kv + h : per_kv + h + 1]
            best = jnp.maximum(top, old_top)
            now, old = jnp.exp2(top - best), jnp.exp2(old_top - best)
            total = acc[:, HD:] * now + old_total * old
            summed = acc[:, :HD] * now + acc_ref[:, c] * old
            o_ref[:, c] = (summed / total).astype(jnp.bfloat16)

    whole = lambda a: pl.BlockSpec(a.shape, lambda i: (0, 0))
    by_row = lambda n: pl.BlockSpec((rows, n), lambda i: (i, 0))
    part = pl.BlockSpec((2 * own, HD), lambda i: (pre // own, 0))
    return pl.pallas_call(
        kernel,
        grid=(steps,),
        in_specs=[
            pl.BlockSpec((rows, width), lambda i: (i, kv_head)),
            by_row(window),
            whole(src_row),
            by_row(width),
            by_row(HD),
        ]
        + [part] * lead
        + [whole(p) for p in pieces],
        out_specs=by_row(width),
        out_shape=jax.ShapeDtypeStruct((LIVE, width), jnp.bfloat16),
        scratch_shapes=[pltpu.VMEM((CMAX + LIVE, HD), jnp.bfloat16)] * 2,
        compiler_params=pltpu.CompilerParams(
            dimension_semantics=("arbitrary",), vmem_limit_bytes=VMEM
        ),
        name="attend_rest",
    )(q, bias, src_row, *carry, *firsts, *pieces)


def gather(table, rows):
    def kernel(table_ref, x_ref, o_ref, sem):
        for j in range(SLOTS):
            pltpu.make_async_copy(
                x_ref.at[pl.ds(pl.multiple_of(table_ref[j] * BLK, BLK), BLK), :],
                o_ref.at[pl.ds(j * BLK, BLK), :],
                sem,
            ).start()
        pltpu.make_async_copy(x_ref.at[pl.ds(0, LIVE), :], o_ref, sem).wait()

    return pl.pallas_call(
        kernel,
        in_specs=[
            pl.BlockSpec(memory_space=pltpu.SMEM),
            pl.BlockSpec(memory_space=pl.ANY),
        ],
        out_specs=pl.BlockSpec(memory_space=pltpu.VMEM),
        out_shape=jax.ShapeDtypeStruct((LIVE, rows.shape[1]), rows.dtype),
        scratch_shapes=[pltpu.SemaphoreType.DMA],
        compiler_params=pltpu.CompilerParams(vmem_limit_bytes=VMEM),
        name="gather",
    )(table, rows)


def finish(order, mine, col, far):
    width = far.shape[-1]
    tile = min(512, width)

    def kernel(order_ref, mine_ref, far_ref, o_ref):
        both = mine_ref[0].astype(jnp.float32) + far_ref[0].astype(jnp.float32)
        o_ref[...] = dot_nn(order_ref[...], both.astype(jnp.bfloat16)).astype(jnp.bfloat16)

    return pl.pallas_call(
        kernel,
        grid=(width // tile,),
        in_specs=[
            pl.BlockSpec((LIVE, LIVE), lambda n: (0, 0)),
            pl.BlockSpec((1, LIVE, tile), lambda n: (0, 0, col // tile + n)),
            pl.BlockSpec((1, LIVE, tile), lambda n: (0, 0, n)),
        ],
        out_specs=pl.BlockSpec((LIVE, tile), lambda n: (0, n)),
        out_shape=jax.ShapeDtypeStruct((LIVE, width), jnp.bfloat16),
        compiler_params=pltpu.CompilerParams(
            dimension_semantics=("arbitrary",), vmem_limit_bytes=VMEM
        ),
        name="finish",
    )(order, mine, far)


def after(value, token):
    return lax.optimization_barrier((value, token))[0]


def project(contexts, weight, blocks, tile, extras, wide):
    groups, tiles = blocks.shape
    count = len(contexts)
    depth = contexts[0].shape[1]

    def kernel(blocks_ref, *refs):
        ctx = refs[:count]
        weights = refs[count : 2 * count]
        more = refs[2 * count : -1]
        o_ref = refs[-1]
        acc = dot_nn(ctx[0][...], weights[0][...])
        for c, w in zip(ctx[1:], weights[1:]):
            acc = acc + dot_nn(c[...], w[...])
        acc = acc.astype(jnp.bfloat16)
        if more:
            acc = acc.astype(jnp.float32)
            for r in more:
                acc = acc + r[0].astype(jnp.float32)
        o_ref[0] = acc.astype(o_ref.dtype)

    def weight_spec(i):
        return pl.BlockSpec((depth, tile), lambda g, n, b: (i, b[g, n]))

    def extra_spec(lead, col):
        return pl.BlockSpec((1, LIVE, tile), lambda g, n, b: (lead + g, 0, col + n))

    return pl.pallas_call(
        kernel,
        grid_spec=pltpu.PrefetchScalarGridSpec(
            num_scalar_prefetch=1,
            grid=(groups, tiles),
            in_specs=[pl.BlockSpec((LIVE, depth), lambda g, n, b: (0, 0))] * count
            + [weight_spec(i) for i in range(count)]
            + [extra_spec(lead, col) for _, lead, col in extras],
            out_specs=pl.BlockSpec((1, LIVE, tile), lambda g, n, b: (g, 0, n)),
        ),
        out_shape=jax.ShapeDtypeStruct(
            (groups, LIVE, tiles * tile), jnp.float32 if wide else jnp.bfloat16
        ),
        compiler_params=pltpu.CompilerParams(
            dimension_semantics=("arbitrary", "arbitrary"), vmem_limit_bytes=VMEM
        ),
        name="project",
    )(blocks, *contexts, *[weight] * count, *[e for e, _, _ in extras])


def local(
    queries,
    comp_keys,
    comp_values,
    prefix_keys,
    prefix_values,
    lengths,
    routing,
    residual,
    out_weight,
):
    tp_count = lax.axis_size("tp")
    bulk_count = lax.axis_size("bulk")
    me = lax.axis_index("tp")
    group_size = HEADS // KVH
    heads_loc = HEADS // tp_count
    kv_local = max(1, heads_loc // group_size)
    per_kv = heads_loc // kv_local
    cap = SLOTS // bulk_count
    width_loc = residual.shape[1]
    pre = prefix_keys.shape[1]
    own = comp_keys.shape[0]

    shelf = jnp.concatenate([prefix_keys[0], prefix_values[0], comp_keys, comp_values], 0)

    def piece(peer, inner):
        col = ((peer * heads_loc) // group_size + inner) * HD
        return lax.dynamic_slice(shelf, (0, col), (shelf.shape[0], HD))

    pieces = []
    for inner in range(kv_local):
        got = [piece(me, inner)]
        for r in range(1, tp_count):
            got.append(
                lax.ppermute(piece(me ^ r, inner), "tp", [(t, t ^ r) for t in range(tp_count)])
            )
        pieces.append(got)

    lens = lengths.reshape(GROUP, 1)
    spans = (lens + BLK - 1) // BLK * BLK
    ids = jnp.arange(GROUP, dtype=jnp.int32)
    first = jnp.sum(
        jnp.where(ids[None, :] < ids[:, None], spans.reshape(1, GROUP), 0), axis=1, keepdims=True
    )

    def packed_of(row):
        hit = ids[:, None] == row // CMAX
        base = jnp.sum(jnp.where(hit, first, 0), axis=0, keepdims=True)
        span = jnp.sum(jnp.where(hit, spans, 0), axis=0, keepdims=True)
        inside = row % CMAX
        return jnp.where(inside < span, base + inside, -1)

    home = jnp.arange(HOME, dtype=jnp.int32)[None, :]
    live = jnp.arange(LIVE, dtype=jnp.int32)
    packed_near = packed_of((home // own ^ me) * own + home % own)

    within = (live[None, :] >= first) & (live[None, :] < first + lens)
    valid = jnp.any(within, axis=0, keepdims=True)
    route = routing.reshape(SLOTS)
    slot = jnp.arange(SLOTS, dtype=jnp.int32)
    before = (route[:, None] == route[None, :]) & (slot[None, :] < slot[:, None])
    place = route[:, None] * cap + jnp.sum(before, axis=1, keepdims=True, dtype=jnp.int32)
    place_row = jnp.sum(
        jnp.where(slot[:, None] == live[None, :] // BLK, place, 0), axis=0, keepdims=True
    )
    place_row = jnp.where(valid, place_row * BLK + live[None, :] % BLK, -1)
    order = (live[:, None] == place_row).astype(jnp.bfloat16)

    origin = jnp.max(
        jnp.where(first.reshape(1, GROUP) <= live[:, None], first.reshape(1, GROUP), 0),
        axis=1,
        keepdims=True,
    )
    window = ATT_ROWS + CMAX
    key_at = (live // ATT_ROWS * ATT_ROWS - CMAX)[:, None] + jnp.arange(window, dtype=jnp.int32)
    bias = jnp.where((key_at >= origin) & (key_at <= live[:, None]), 0.0, NEG)

    block = jnp.arange(HOME // BLK, dtype=jnp.int32)[None, :]
    found = packed_of(block * BLK) == slot[:, None] * BLK
    table = jnp.sum(jnp.where(found, block, 0), axis=1, dtype=jnp.int32)
    query = gather(table, queries)
    early = max(1, tp_count // 2)
    carries = [
        attend_first(query, pieces[n][:early], pre, n, per_kv) for n in range(kv_local)
    ]
    contexts = [
        attend_rest(
            query,
            bias,
            packed_near,
            carries[n],
            pieces[n][:early],
            pieces[n][early:],
            pre,
            own,
            n,
            per_kv,
        )
        for n in range(kv_local)
    ]

    def send_home(rows):
        return lax.all_to_all(
            rows.reshape(bulk_count, -1, rows.shape[-1]),
            "bulk",
            split_axis=0,
            concat_axis=0,
            tiled=True,
        ).reshape(rows.shape)

    chunks = CHUNKS if tp_count == 4 else 1
    part = width_loc // chunks
    tile = min(512, part)
    tiles = part // tile
    per_dev = width_loc // tile
    if tp_count != 4:
        base = jnp.arange(tp_count * per_dev, dtype=jnp.int32)[None, :]
        full = project(contexts, out_weight, base, tile, [], False)[0]
        summed = lax.psum_scatter(full, "tp", scatter_dimension=1, tiled=True)
        return send_home(finish(order, gather(table, residual)[None], 0, summed[None]))

    swap = [(t, t ^ 1) for t in range(tp_count)]
    cross = [(t, t ^ 2) for t in range(tp_count)]

    token = contexts[-1]

    def run(j, rels, extras):
        ids = j * tiles + jnp.arange(tiles, dtype=jnp.int32)
        blocks = jnp.stack([(me ^ r) * per_dev + ids for r in rels])
        return project(after(contexts, token), out_weight, blocks, tile, extras, False)

    away, far, mine, kept = {}, {}, {}, None
    homes = []
    for name in PLAN:
        what, j = name[:4].rstrip("0123456789"), int(name[-1]) if name[-1].isdigit() else 0
        if what == "away":
            token = run(j, (1, 3), [])
        elif what == "kept":
            token = kept = gather(table, after(residual, token))
        elif what == "far":
            token = run(j, (2,), [(away[j], 1, 0)])
        elif what == "mine":
            token = mine[j] = run(j, (0,), [(away[j], 0, 0), (kept[None], 0, j * tiles)])
        else:
            token = finish(order, after(mine[j], token), 0, far[j])
        if what == "away":
            away[j] = lax.ppermute(token, "tp", swap)
        elif what == "far":
            far[j] = lax.ppermute(token, "tp", cross)
        elif what == "done":
            homes.append(send_home(token))
    out = after(jnp.zeros((LIVE, width_loc), jnp.bfloat16), token)
    for j in range(chunks):
        out = lax.dynamic_update_slice(out, homes[j], (0, j * part))
    return out


def solution(mesh):
    return jax.shard_map(
        local,
        mesh=mesh,
        in_specs=(
            P("bulk", "tp"),
            P(("bulk", "tp"), None),
            P(("bulk", "tp"), None),
            P("bulk", "tp", None),
            P("bulk", "tp", None),
            P("bulk", None),
            P("bulk", None),
            P("bulk", "tp"),
            P("tp", None),
        ),
        out_specs=P("bulk", "tp"),
        check_vma=False,
    )
```
